1024 devices in a mesh: pipe: 16 (over y, x), dp: 64 (over z, core).
Axes of the slice: x: 4, y: 4, z: 32, core: 2. Of those that a mesh axis runs over, the one named last changes fastest.
Arguments:
- layer_inputs: bfloat16 [2, 8192, 16384], P(None, 'dp', 'pipe'), may hold values from -6 to 6
- top_grad: bfloat16 [2, 8192, 2048], P(None, 'dp'), may hold values from -6 to 6
- a_weight: bfloat16 [16384, 512], P('pipe'), may hold values from -0.125 to 0.125
- b_weight: bfloat16 [512, 16384], P(None, 'pipe'), may hold values from -0.25 to 0.25
- master: float32 [512, 16384], P('dp', 'pipe'), may hold values from -0.25 to 0.25
- first_moment: float32 [512, 16384], P('dp', 'pipe'), may hold values from -6 to 6
- second_moment: float32 [512, 16384], P('dp', 'pipe'), may hold values from 0.5 to 4
- step_count: int32 [1], replicated, may hold values from 1 to 16
Outputs:
- input_grads: bfloat16 [2, 8192, 16384], P(None, 'dp', 'pipe')
- new_master: float32 [512, 16384], P('dp', 'pipe')
- new_first: float32 [512, 16384], P('dp', 'pipe')
- new_second: float32 [512, 16384], P('dp', 'pipe')
- new_weight: bfloat16 [512, 16384], P(None, 'pipe')
The draws below stay inside these ranges and needn't reach their ends.
All inputs are finite; a program needn't handle non-finite values.
Results may differ from the reference program's by a relative error of at most 0.023.
Values may be sent and summed in bfloat16 or wider, within the bound.
No kernel may reach another device: no remote copies, remote signals or barrier semaphores. Data moves between devices by JAX's collectives and lax.ppermute only.
A program may use at most 32 MiB of HBM per device.

```python
import math
import jax
import jax.numpy as jnp
from jax import lax

D = 2048
R = 512
MICRO = 2
SECTIONS = 8
TOKENS = 8192
N_PIPE = 16


def shard_levels(own_key, extent, split, low, top_value):
    level, own = 1.0, jax.random.fold_in(own_key, 6)
    for axis_at, blocks in split:
        heights = jnp.exp(jax.random.uniform(jax.random.fold_in(own, axis_at), (blocks,), jnp.float32, low / len(split), top_value / len(split)))
        level = level * jnp.repeat(heights, extent[axis_at] // blocks).reshape([-1 if axis == axis_at else 1 for axis in range(len(extent))])
    return level


def gaussian(own_key, extent, scale, most, split=(), dtype=jnp.bfloat16):
    gain = shard_levels(own_key, extent, split, -0.22, 0.18) if split else 1.0
    drawn = jax.random.normal(own_key, extent, jnp.float32) * scale * gain
    return jnp.minimum(jnp.maximum(drawn, -most), most).astype(dtype)


def setup_inputs(seed: int = 0) -> dict:
    seeds = jax.random.split(jax.random.key(seed), 9)
    layer_inputs = gaussian(seeds[0], (MICRO, TOKENS, SECTIONS * D), 1.0, 6.0, ((1, 64), (2, 16)))
    top_grad = gaussian(seeds[1], (MICRO, TOKENS, D), 1.0, 6.0, ((1, 64),))
    a_weight = gaussian(seeds[2], (SECTIONS * D, R), D ** -0.5, 0.125, ((0, 16),))
    b_weight = gaussian(seeds[3], (R, SECTIONS * D), R ** -0.5, 0.25, ((1, 16),))
    master = gaussian(seeds[4], (R, SECTIONS * D), R ** -0.5, 0.25, ((0, 64), (1, 16)), jnp.float32)
    first_moment = gaussian(seeds[5], (R, SECTIONS * D), 1.0, 6.0, ((0, 64), (1, 16)), jnp.float32)
    second_moment = jnp.clip(jnp.exp(math.log(4.0) - 2.0794415 * jax.random.uniform(seeds[6], (R, SECTIONS * D), jnp.float32) ** shard_levels(seeds[6], (R, SECTIONS * D), ((0, 64), (1, 16)), -0.2, 0.2)), 0.5, 4.0)
    step_count = jax.random.randint(seeds[7], (1,), 1, 17).astype(jnp.int32)
    return dict(layer_inputs=layer_inputs, top_grad=top_grad, a_weight=a_weight, b_weight=b_weight, master=master, first_moment=first_moment, second_moment=second_moment, step_count=step_count)


beta_one = 0.9
beta_two = 0.95
epsilon = 1e-08
learn_rate = 0.05
grad_scale = 0.125

def silu_slope(pre_act):
    sigmoid = jax.nn.sigmoid(pre_act)
    return sigmoid * (1.0 + pre_act * (1.0 - sigmoid))

def adam_update(gradient, master, first_moment, second_moment, step_count):
    count = step_count[0].astype(jnp.float32)
    new_first = beta_one * first_moment + (1.0 - beta_one) * gradient
    new_second = beta_two * second_moment + (1.0 - beta_two) * gradient * gradient
    first_fix = 1.0 - jnp.power(beta_one, count)
    second_fix = 1.0 - jnp.power(beta_two, count)
    new_master = master - learn_rate * (new_first / first_fix) / (jnp.sqrt(new_second / second_fix) + epsilon)
    return (new_master, new_first, new_second)

def reference(layer_inputs, top_grad, a_weight, b_weight, master, first_moment, second_moment, step_count):
    sections = N_PIPE // 2
    half_width = D // 2
    all_rows = MICRO * TOKENS
    upstream = top_grad.reshape(all_rows, D)
    grad_blocks = []
    weight_blocks = []
    for section_id in reversed(range(sections)):
        offset = section_id * D
        inputs = layer_inputs[:, :, offset:offset + D].reshape(all_rows, D)
        pre_act = jnp.zeros((all_rows, R), jnp.float32)
        branch = jnp.zeros((all_rows, R), jnp.float32)
        for half_id in range(2):
            start_col = half_id * half_width
            rows_here = a_weight[offset + start_col:offset + start_col + half_width]
            partial_value = jnp.dot(inputs[:, start_col:start_col + half_width], rows_here, preferred_element_type=jnp.float32).astype(jnp.bfloat16)
            pre_act = pre_act + lax.optimization_barrier(partial_value).astype(jnp.float32)
            cols_here = b_weight[:, offset + start_col:offset + start_col + half_width]
            branch_part = jnp.dot(upstream[:, start_col:start_col + half_width], cols_here.T, preferred_element_type=jnp.float32).astype(jnp.bfloat16)
            branch = branch + lax.optimization_barrier(branch_part).astype(jnp.float32)
        hidden = jax.nn.silu(pre_act).astype(jnp.bfloat16)
        grad_pre = (branch * silu_slope(pre_act)).astype(jnp.bfloat16)
        new_halves = []
        grad_halves = []
        for half_id in range(2):
            start_col = half_id * half_width
            rows_here = a_weight[offset + start_col:offset + start_col + half_width]
            upstream_half = upstream[:, start_col:start_col + half_width]
            back_term = jnp.dot(grad_pre, rows_here.T, preferred_element_type=jnp.float32)
            new_halves.append((upstream_half.astype(jnp.float32) + back_term).astype(jnp.bfloat16))
            grad_halves.append(jnp.dot(hidden.T, upstream_half, preferred_element_type=jnp.float32))
        new_upstream = jnp.concatenate(new_halves, axis=1)
        grad_blocks.insert(0, new_upstream)
        weight_blocks.insert(0, jnp.concatenate(grad_halves, axis=1))
        upstream = new_upstream
    input_grads = jnp.concatenate(grad_blocks, axis=1).reshape(MICRO, TOKENS, sections * D)
    gradient = jnp.concatenate(weight_blocks, axis=1) * grad_scale
    new_master, new_first, new_second = adam_update(gradient, master, first_moment, second_moment, step_count)
    return (input_grads, new_master, new_first, new_second, new_master.astype(jnp.bfloat16))
```

```python
import jax
import jax.numpy as jnp
from jax import lax
from jax.sharding import PartitionSpec as P

beta_one = 0.9
beta_two = 0.95
epsilon = 1e-08
learn_rate = 0.05
grad_scale = 0.125

CHUNKS = 4
STREAMS = 2
NEAR = 4
CORES = 2


def swapped(x, axis, bit):
    return lax.ppermute(x, axis, [(i, i ^ 1 << bit) for i in range(lax.axis_size(axis))])


def passed_along(block, axis, distance):
    devices = range(lax.axis_size(axis))
    route = [(i - distance, i) for i in devices if i - distance in devices]
    return lax.ppermute(block, axis, route)


def silu_slope(pre_act):
    sigmoid = jax.nn.sigmoid(pre_act)
    return sigmoid * (1.0 + pre_act * (1.0 - sigmoid))


def adam_update(gradient, master, first_moment, second_moment, step_count):
    count = step_count[0].astype(jnp.float32)
    new_first = beta_one * first_moment + (1.0 - beta_one) * gradient
    new_second = beta_two * second_moment + (1.0 - beta_two) * gradient * gradient
    first_fix = 1.0 - jnp.power(beta_one, count)
    second_fix = 1.0 - jnp.power(beta_two, count)
    new_master = master - learn_rate * (new_first / first_fix) / (
        jnp.sqrt(new_second / second_fix) + epsilon
    )
    return (new_master, new_first, new_second)


def dp_groups(dp_size):
    far_size = dp_size // (NEAR * CORES)
    at = lambda far, near, core: (far * NEAR + near) * CORES + core
    near_groups = [
        [at(far, near, core) for near in range(NEAR)]
        for far in range(far_size)
        for core in range(CORES)
    ]
    far_groups = [
        [at(far, near, core) for far in range(far_size)]
        for near in range(NEAR)
        for core in range(CORES)
    ]
    return far_size, near_groups, far_groups


def scattered_sum(partial):
    dp_size = lax.axis_size("dp")
    far_size, near_groups, far_groups = dp_groups(dp_size)
    core = lax.axis_index("dp") % CORES
    rows, width = partial.shape
    block = rows // dp_size
    blocks = partial.reshape(far_size, NEAR, CORES, block, width)
    kept = lax.dynamic_index_in_dim(blocks, core, 2, keepdims=False)
    sent = lax.dynamic_index_in_dim(blocks, 1 - core, 2, keepdims=False).astype(jnp.bfloat16)
    half = kept + swapped(sent, "dp", 0).astype(jnp.float32)
    half = half.astype(jnp.bfloat16).transpose(1, 0, 2, 3)
    near = lax.all_to_all(half, "dp", 0, 0, axis_index_groups=near_groups, tiled=True)
    quarter = jnp.sum(near.astype(jnp.float32), axis=0).astype(jnp.bfloat16)
    far = lax.all_to_all(quarter, "dp", 0, 0, axis_index_groups=far_groups, tiled=True)
    return jnp.sum(far.astype(jnp.float32), axis=0)


def gathered(own):
    dp_size = lax.axis_size("dp")
    far_size, near_groups, far_groups = dp_groups(dp_size)
    core = lax.axis_index("dp") % CORES
    block, width = own.shape
    copies = jnp.broadcast_to(own[None], (far_size, block, width))
    far = lax.all_to_all(copies, "dp", 0, 0, axis_index_groups=far_groups, tiled=True)
    copies = jnp.broadcast_to(far[None], (NEAR, far_size, block, width))
    near = lax.all_to_all(copies, "dp", 0, 0, axis_index_groups=near_groups, tiled=True)
    other = swapped(near, "dp", 0)
    first = jnp.where(core == 0, near, other)
    second = jnp.where(core == 0, other, near)
    whole = jnp.stack([first, second], axis=2)
    return whole.transpose(1, 0, 2, 3, 4).reshape(dp_size * block, width)


def per_device(
    layer_inputs, top_grad, a_weight, b_weight, master, first_moment, second_moment, step_count
):
    sections = lax.axis_size("pipe") // 2
    position = lax.axis_index("pipe")
    section_id = position // 2
    half_id = position % 2
    micro_count, token_rows, half_width = layer_inputs.shape
    inner_width = a_weight.shape[1]
    all_rows = micro_count * token_rows
    chunk_rows = all_rows // CHUNKS
    per_stream = CHUNKS // STREAMS
    last_section = section_id == sections - 1

    inputs = layer_inputs.reshape(all_rows, half_width)
    own_part = jnp.dot(inputs, a_weight, preferred_element_type=jnp.float32).astype(jnp.bfloat16)
    pair_part = swapped(own_part, "pipe", 0)
    pre_act = own_part.astype(jnp.float32) + pair_part.astype(jnp.float32)
    slope = silu_slope(pre_act)
    hidden = jax.nn.silu(pre_act).astype(jnp.bfloat16)
    upstream_all = lax.dynamic_slice_in_dim(top_grad, half_id * half_width, half_width, 2)
    upstream_all = upstream_all.reshape(all_rows, half_width)

    def chunk_of(x, chunk):
        return x[chunk * chunk_rows : (chunk + 1) * chunk_rows]

    grads_out = [None] * CHUNKS
    upstream_seen = [None] * CHUNKS
    empty = jnp.zeros((chunk_rows, half_width), jnp.bfloat16)
    carried = [empty] * STREAMS
    for turn in range(sections + per_stream - 1):
        order = turn - (sections - 1 - section_id)
        for stream in range(STREAMS):
            chunks = [stream * per_stream + i for i in range(per_stream)]
            from_top = chunk_of(upstream_all, chunks[min(turn, per_stream - 1)])
            upstream = jnp.where(last_section, from_top, carried[stream])
            part = lax.dot_general(
                upstream, b_weight, (((1,), (1,)), ((), ())), preferred_element_type=jnp.float32
            ).astype(jnp.bfloat16)
            other = swapped(part, "pipe", 0)
            branch = part.astype(jnp.float32) + other.astype(jnp.float32)
            local_slope = chunk_of(slope, chunks[0])
            for i in range(1, per_stream):
                local_slope = jnp.where(order == i, chunk_of(slope, chunks[i]), local_slope)
            grad_pre = (branch * local_slope).astype(jnp.bfloat16)
            back_term = lax.dot_general(
                grad_pre, a_weight, (((1,), (1,)), ((), ())), preferred_element_type=jnp.float32
            )
            grad_in = (upstream.astype(jnp.float32) + back_term).astype(jnp.bfloat16)
            if turn < sections + per_stream - 2:
                carried[stream] = passed_along(grad_in, "pipe", -2)
            for i, chunk in enumerate(chunks):
                if not i <= turn <= i + sections - 1:
                    continue
                if grads_out[chunk] is None:
                    grads_out[chunk] = grad_in
                    upstream_seen[chunk] = upstream
                else:
                    grads_out[chunk] = jnp.where(order == i, grad_in, grads_out[chunk])
                    upstream_seen[chunk] = jnp.where(order == i, upstream, upstream_seen[chunk])

    upstream_seen = jnp.concatenate(upstream_seen, axis=0)
    grads_out = jnp.concatenate(grads_out, axis=0).reshape(layer_inputs.shape)
    partial = lax.dot_general(
        hidden, upstream_seen, (((0,), (0,)), ((), ())), preferred_element_type=jnp.float32
    )
    gradient = scattered_sum(partial) * grad_scale
    new_master, new_first, new_second = adam_update(
        gradient, master, first_moment, second_moment, step_count
    )
    new_weight = gathered(new_master.astype(jnp.bfloat16))
    return (grads_out, new_master, new_first, new_second, new_weight)


def solution(mesh):
    return jax.shard_map(
        per_device,
        mesh=mesh,
        in_specs=(
            P(None, "dp", "pipe"),
            P(None, "dp", None),
            P("pipe", None),
            P(None, "pipe"),
            P("dp", "pipe"),
            P("dp", "pipe"),
            P("dp", "pipe"),
            P(),
        ),
        out_specs=(
            P(None, "dp", "pipe"),
            P("dp", "pipe"),
            P("dp", "pipe"),
            P("dp", "pipe"),
            P(None, "pipe"),
        ),
        check_vma=False,
    )
```
